32 devices in a mesh: seq: 32 (over z, y, x, core), head: 1.
Axes of the slice: x: 2, y: 2, z: 4, core: 2. Of those that a mesh axis runs over, the one named last changes fastest.
Arguments:
- queries: float32 [8192, 16, 256], P('seq', 'head'), may hold values from -6 to 6
- key_rows: float32 [8192, 256], P(('seq', 'head')), may hold values from -6 to 6
- value_rows: float32 [8192, 256], P(('seq', 'head')), may hold values from -6 to 6
- forward_out: float32 [8192, 16, 256], P('seq', 'head'), may hold values from -6 to 6
- out_grad: float32 [8192, 16, 256], P('seq', 'head'), may hold values from -6 to 6
- log_norm: float32 [8192, 16], P('seq', 'head'), may hold values from 6 to 9
- doc_ids: int32 [8192], P(('seq', 'head')), may hold values from 0 to 3, never falling along the last dimension, each value on 1 to 4096 neighbouring positions
Outputs:
- grad_queries: float32 [8192, 16, 256], P('seq', 'head')
- grad_keys: float32 [8192, 256], P(('seq', 'head'))
- grad_values: float32 [8192, 256], P(('seq', 'head'))
The draws below stay inside these ranges and needn't reach their ends.
Inputs may be any that keep to these rules, and one draw needn't show every extreme that they name: `doc_ids`: never falling along the tokens; each document holds 1 to 4096 tokens, one exactly 4096.
All inputs are finite; a program needn't handle non-finite values.
Results may differ from the reference program's by a relative error of at most 0.0003.
Values sent between devices are 32-bit elements; how exact they have to be, the bound alone decides.
No kernel may reach another device: no remote copies, remote signals or barrier semaphores. Data moves between devices by JAX's collectives and lax.ppermute only.
A program may use at most 128 MiB of HBM per device.

```python
import math
import jax
import jax.numpy as jnp
import numpy as np
from jax import lax

HEAD_DIM = 256
HEADS = 16
WIN = 2048
ROWS = 256
TOKENS = 8192
DOCS = 4
DOC_MOST = 4096


def block_levels(stream_key, shape, cuts, low, top_value):
    def one(dim, parts):
        steps = jax.random.uniform(jax.random.fold_in(jax.random.fold_in(stream_key, 6), dim), (parts,), jnp.float32, low / len(cuts), top_value / len(cuts))
        return jnp.repeat(jnp.exp(steps), shape[dim] // parts).reshape((-1,) + (1,) * (len(shape) - dim - 1))

    loudness = one(*cuts[0])
    for cut in cuts[1:]:
        loudness = loudness * one(*cut)
    return loudness


def split_up(number_of, total, limit, slope):
    portions = [(1 << 20) // math.isqrt(grade ** slope) + 1 for grade in range(2, number_of + 1)]
    spare, holding = total - limit - (number_of - 1), [1] * (number_of - 1)
    while spare > 0:
        free = [i for i in range(number_of - 1) if holding[i] < limit]
        whole, budget = sum([portions[i] for i in free]), spare
        for i in free:
            more = min(limit - holding[i], max(1, budget * portions[i] // whole), spare)
            holding[i] = holding[i] + more
            spare = spare - more
    return np.array([limit] + holding)


def ragged(stream_key, number_of, total, bound, slope):
    if number_of == 2:
        one = jax.random.randint(stream_key, (), max(1, total - bound), min(bound, total - 1) + 1)
        return jnp.stack([one, total - one])
    tallies = jnp.asarray(split_up(number_of, total, bound, slope), jnp.int32)
    couples = (number_of - 1) // 2
    source_of, sink = tallies[1:1 + 2 * couples:2], tallies[2:2 + 2 * couples:2]
    margin = jnp.minimum(source_of - 1, bound - sink)
    shifted = jax.random.randint(jax.random.fold_in(stream_key, 1), (couples,), 0, 1 << 20) % (margin + 1)
    tallies = tallies.at[1:1 + 2 * couples:2].set(source_of - shifted).at[2:2 + 2 * couples:2].set(sink + shifted)
    return tallies[jax.random.permutation(jax.random.fold_in(stream_key, 2), number_of)]


def noise(stream_key, shape, spread, most, pieces=(), kind=jnp.bfloat16):
    entries = spread * jax.random.normal(stream_key, shape, jnp.float32)
    if pieces:
        entries = entries * block_levels(stream_key, shape, pieces, -0.22, 0.18)
    return jnp.clip(entries, -most, most).astype(kind)


def setup_inputs(seed: int = 0) -> dict:
    streams_of = jax.random.split(jax.random.key(seed), 8)
    return {
        "queries": noise(streams_of[0], (TOKENS, HEADS, HEAD_DIM), 1.0, 6.0, ((0, 32),), jnp.float32),
        "key_rows": noise(streams_of[1], (TOKENS, HEAD_DIM), 1.0, 6.0, ((0, 32),), jnp.float32),
        "value_rows": noise(streams_of[2], (TOKENS, HEAD_DIM), 1.0, 6.0, ((0, 32),), jnp.float32),
        "forward_out": noise(streams_of[3], (TOKENS, HEADS, HEAD_DIM), 1.0, 6.0, ((0, 32),), jnp.float32),
        "out_grad": noise(streams_of[4], (TOKENS, HEADS, HEAD_DIM), 1.0, 6.0, ((0, 32),), jnp.float32),
        "log_norm": jnp.clip(6.0 + 3.0 * jax.random.uniform(streams_of[5], (TOKENS, HEADS), jnp.float32) ** block_levels(streams_of[5], (TOKENS, HEADS), ((0, 32),), -0.2, 0.2), 6.0, 9.0),
        "doc_ids": jnp.searchsorted(jnp.cumsum(ragged(streams_of[6], DOCS, TOKENS, DOC_MOST, 1)), jnp.arange(TOKENS), side="right").astype(jnp.int32),
    }


def reference(queries, key_rows, value_rows, forward_out, out_grad, log_norm, doc_ids):
    factor = HEAD_DIM ** -0.5
    extent = WIN + ROWS
    blocks = TOKENS // ROWS
    high = lax.Precision.HIGHEST
    pad_rows = jnp.zeros((WIN, HEAD_DIM), key_rows.dtype)
    keys_pad = jnp.concatenate([pad_rows, key_rows], axis=0)
    vals_pad = jnp.concatenate([pad_rows, value_rows], axis=0)
    ids_pad = jnp.concatenate([jnp.full((WIN,), -1, jnp.int32), doc_ids.astype(jnp.int32)], axis=0)

    def advance(carry, block):
        keys_grad, vals_grad = carry
        start = (block * ROWS).astype(jnp.int32)
        query_blk = lax.dynamic_slice_in_dim(queries, start, ROWS, 0)
        out_blk = lax.dynamic_slice_in_dim(forward_out, start, ROWS, 0)
        grad_blk = lax.dynamic_slice_in_dim(out_grad, start, ROWS, 0)
        norm_blk = lax.dynamic_slice_in_dim(log_norm, start, ROWS, 0)
        query_ids = lax.dynamic_slice_in_dim(doc_ids, start, ROWS, 0)
        key_blk = lax.dynamic_slice_in_dim(keys_pad, start, extent, 0)
        val_blk = lax.dynamic_slice_in_dim(vals_pad, start, extent, 0)
        key_ids = lax.dynamic_slice_in_dim(ids_pad, start, extent, 0)
        query_pos = start + jnp.arange(ROWS, dtype=jnp.int32)
        key_pos = start - WIN + jnp.arange(extent, dtype=jnp.int32)
        distance = query_pos[:, None] - key_pos[None, :]
        allowed = (distance >= 0) & (distance < WIN) & (query_ids[:, None] == key_ids[None, :]) & (key_pos[None, :] >= 0)
        scores = jnp.einsum("rhd,kd->hrk", query_blk, key_blk, precision=high) * factor
        probs = jnp.where(allowed[None], jnp.exp(scores - norm_blk.T[:, :, None]), 0.0)
        vals_blk_grad = jnp.einsum("hrk,rhd->kd", probs, grad_blk, precision=high)
        grad_probs = jnp.einsum("rhd,kd->hrk", grad_blk, val_blk, precision=high)
        delta = jnp.sum(grad_blk * out_blk, axis=-1)
        grad_scores = probs * (grad_probs - delta.T[:, :, None])
        query_grad = jnp.einsum("hrk,kd->rhd", grad_scores, key_blk, precision=high) * factor
        keys_blk_grad = jnp.einsum("hrk,rhd->kd", grad_scores, query_blk, precision=high) * factor
        keys_grad = lax.dynamic_update_slice_in_dim(keys_grad, lax.dynamic_slice_in_dim(keys_grad, start, extent, 0) + keys_blk_grad, start, 0)
        vals_grad = lax.dynamic_update_slice_in_dim(vals_grad, lax.dynamic_slice_in_dim(vals_grad, start, extent, 0) + vals_blk_grad, start, 0)
        return (keys_grad, vals_grad), query_grad

    start_carry = (jnp.zeros_like(keys_pad), jnp.zeros_like(vals_pad))
    (keys_grad, vals_grad), query_grads = lax.scan(advance, start_carry, jnp.arange(blocks, dtype=jnp.int32))
    grad_queries = query_grads.reshape(TOKENS, HEADS, HEAD_DIM)
    return grad_queries, keys_grad[WIN:], vals_grad[WIN:]
```

```python
import functools
import math

import jax
import jax.numpy as jnp
from jax import lax
from jax.experimental import pallas as pl
from jax.experimental.pallas import tpu as pltpu
from jax.sharding import PartitionSpec as P

WIN = 2048
TILE = 256
LOG2E = math.log2(math.e)
LN2 = math.log(2.0)
MASKED = -1e30
NN = (((1,), (0,)), ((), ()))
NT = (((1,), (1,)), ((), ()))
F32 = jnp.float32
BF16 = jnp.bfloat16


def shifted(value, axis, steps):
    count = lax.axis_size(axis)
    leading, last = (max(0, -steps), min(count, count - steps))
    return lax.ppermute(value, axis, [(source, source + steps) for source in range(leading, last)])


def dot(a, b, dims):
    return lax.dot_general(a, b, dims, preferred_element_type=F32)


def halves(x):
    high = x.astype(BF16)
    return high, (x - high.astype(F32)).astype(BF16)


def kernel(blocks, slab_count, rows, has_sum, *refs):
    q_ref, g_ref, vec_ref, *rest = refs
    slabs, rest = rest[:slab_count], rest[slab_count:]
    sum_ref, rest = (rest[0], rest[1:]) if has_sum else (None, rest)
    dq_ref, rest = rest[0], rest[1:]
    outs, rest = rest[:slab_count], rest[slab_count:]
    k_hi, k_lo, kt_hi, kt_lo, v_hi, v_lo, dk_acc, dv_acc, first_ref = rest
    tile = pl.program_id(0)
    width = q_ref.shape[1]

    @pl.when(tile == 0)
    def _():
        dk_acc[...] = jnp.zeros_like(dk_acc)
        dv_acc[...] = jnp.zeros_like(dv_acc)
        for s, slab in enumerate(slabs):
            at = pl.ds(s * rows, rows)
            keys, values = slab[0:rows, :], slab[rows : 2 * rows, :]
            k_hi[at, :], k_lo[at, :] = halves(keys)
            kt_hi[:, at], kt_lo[:, at] = halves(keys.T)
            v_hi[at, :], v_lo[at, :] = halves(values)
            ids = slab[2 * rows :, :]
            same = jnp.where(ids == vec_ref[5:6, 0:1], F32(1), F32(0))
            count = jnp.sum(jnp.sum(same, axis=0, keepdims=True), axis=1, keepdims=True)
            first_ref[s : s + 1, :] = jnp.broadcast_to(rows - count, (1, TILE))

    q_hi, q_lo = halves(q_ref[...] * F32(LOG2E / math.sqrt(width)))
    g_hi, g_lo = halves(g_ref[...])
    log_norm, delta = vec_ref[0:1, :], vec_ref[1:2, :]

    def span(block):
        start, size, _ = block
        if callable(start):
            start = pl.multiple_of(start(tile), 128)
        return pl.ds(start, size), start

    def front(block):
        at, start = span(block)
        scores = dot(k_hi[at, :], q_hi, NT) + dot(k_lo[at, :], q_hi, NT) + dot(k_hi[at, :], q_lo, NT)
        grad_probs = dot(v_hi[at, :], g_hi, NT) + dot(v_lo[at, :], g_hi, NT) + dot(v_hi[at, :], g_lo, NT)
        return scores, grad_probs

    def back(block, scores, grad_probs, dqt):
        at, start = span(block)
        size, both = block[1], block[2]
        row = lax.broadcasted_iota(jnp.int32, (size, TILE), 0).astype(F32)
        if both:
            low = jnp.maximum(vec_ref[2:3, :], first_ref[0:1, :]) - lax.convert_element_type(start, F32)
            high = vec_ref[4:5, :] - lax.convert_element_type(start, F32)
            allowed = (row >= low) & (row <= high)
        else:
            allowed = row >= jnp.maximum(vec_ref[3:4, :], first_ref[start // rows : start // rows + 1, :])
        probs = jnp.exp2(jnp.where(allowed, scores - log_norm, F32(MASKED)))
        grad_scores = probs * (grad_probs - delta)
        p_hi, p_lo = halves(probs)
        s_hi, s_lo = halves(grad_scores)
        dv_acc[at, :] += dot(p_hi, g_hi, NN) + dot(p_lo, g_hi, NN) + dot(p_hi, g_lo, NN)
        dk_acc[at, :] += dot(s_hi, q_hi, NN) + dot(s_lo, q_hi, NN) + dot(s_hi, q_lo, NN)
        new = dot(kt_hi[:, at], s_hi, NN) + dot(kt_lo[:, at], s_hi, NN) + dot(kt_hi[:, at], s_lo, NN)
        return new if dqt is None else dqt + new

    dqt = None
    coming = front(blocks[0])
    for n, block in enumerate(blocks):
        here = coming
        if n + 1 < len(blocks):
            coming = front(blocks[n + 1])
        dqt = back(block, *here, dqt)
    dq = dqt.T * F32(1 / math.sqrt(width))
    dq_ref[...] = dq if sum_ref is None else dq + sum_ref[...]

    @pl.when(tile == pl.num_programs(0) - 1)
    def _():
        for s, out in enumerate(outs):
            at = pl.ds(s * rows, rows)
            out[0:rows, :] = dk_acc[at, :] * F32(LN2)
            out[rows : 2 * rows, :] = dv_acc[at, :]


def attend(blocks, q, g, vec, slabs, rows, dq_sum):
    total, width = q.shape
    count = len(slabs)
    keys = count * rows
    tiles = total // TILE
    tile_spec = pl.BlockSpec((TILE, width), lambda i: (i, 0))
    whole = lambda shape: pl.BlockSpec(shape, lambda i: (0, 0))
    sums = [] if dq_sum is None else [dq_sum]
    computed = sum(b[1] for b in blocks)
    results = pl.pallas_call(
        functools.partial(kernel, blocks, count, rows, bool(sums)),
        grid=(tiles,),
        in_specs=[tile_spec, tile_spec, pl.BlockSpec((8, TILE), lambda i: (0, i))]
        + [whole(slabs[0].shape)] * count
        + [tile_spec] * len(sums),
        out_specs=[tile_spec] + [whole((2 * rows, width))] * count,
        out_shape=[jax.ShapeDtypeStruct((total, width), F32)]
        + [jax.ShapeDtypeStruct((2 * rows, width), F32)] * count,
        scratch_shapes=[
            pltpu.VMEM((keys, width), BF16),
            pltpu.VMEM((keys, width), BF16),
            pltpu.VMEM((width, keys), BF16),
            pltpu.VMEM((width, keys), BF16),
            pltpu.VMEM((keys, width), BF16),
            pltpu.VMEM((keys, width), BF16),
            pltpu.VMEM((keys, width), F32),
            pltpu.VMEM((keys, width), F32),
            pltpu.VMEM((8, TILE), F32),
        ],
        compiler_params=pltpu.CompilerParams(vmem_limit_bytes=48 * 1024 * 1024),
        cost_estimate=pl.CostEstimate(
            flops=30 * total * computed * width, bytes_accessed=12 * total * width, transcendentals=total * computed
        ),
    )(q, g, vec, *slabs, *sums)
    return results[0], results[1:]


def on_device(queries, key_rows, value_rows, forward_out, out_grad, log_norm, doc_ids):
    rows, heads, width = queries.shape
    reach = WIN // rows
    ids = doc_ids.astype(F32) + 1.0
    if lax.axis_size("head") > 1:
        gather = functools.partial(lax.all_gather, axis_name="head", axis=0, tiled=True)
        key_rows, value_rows, ids = gather(key_rows), gather(value_rows), gather(ids)
    id_rows = 8 * pl.cdiv(rows, 8 * width)
    id_part = jnp.pad(ids, (0, id_rows * width - rows)).reshape(id_rows, width)
    own = jnp.concatenate([key_rows, value_rows, id_part], axis=0)
    slab = {0: own}
    for distance in [reach] + list(range(reach - 1, 0, -1)):
        slab[distance] = shifted(own, "seq", distance)

    token = jnp.arange(rows, dtype=F32)
    before = jnp.sum((ids[None, :] < ids[:, None]).astype(F32), axis=1)
    first = before == 0
    per_token = jnp.stack(
        [
            jnp.where(first, token + 1, rows + before),
            jnp.where(first, 0.0, 1e9),
            token + rows,
            jnp.broadcast_to(ids[0], (rows,)),
        ]
    )
    spread = jnp.broadcast_to(per_token[:, :, None], (4, rows, heads)).reshape(4, rows * heads)
    delta = jnp.sum(out_grad * forward_out, axis=-1).reshape(1, -1)
    scaled = (log_norm * F32(LOG2E)).reshape(1, -1)
    vec = jnp.concatenate([scaled, delta, spread, jnp.zeros((2, rows * heads), F32)], axis=0)

    q = queries.reshape(rows * heads, width)
    g = out_grad.reshape(rows * heads, width)
    tokens = TILE // heads
    edge = max(tokens, 128)
    edges = ((lambda i: (i * tokens) // edge * edge, rows + edge, True),)
    back = {}
    dq, (back[reach], own_part) = attend(edges, q, g, vec, [slab[reach], own], rows, None)
    middle = reach // 2
    groups = [list(range(reach - 1, middle - 1, -1)), list(range(middle - 1, 1, -1)), [1]]
    for group in groups:
        blocks = tuple((n * rows, rows, False) for n in range(len(group)))
        dq, parts = attend(blocks, q, g, vec, [slab[d] for d in group], rows, dq)
        back.update(zip(group, parts))
    for distance in [reach] + [d for group in groups for d in group]:
        own_part = own_part + shifted(back[distance], "seq", -distance)
    keys_grad, values_grad = own_part[:rows], own_part[rows:]
    if lax.axis_size("head") > 1:
        keys_grad, values_grad = (
            lax.psum_scatter(x, "head", scatter_dimension=0, tiled=True) for x in (keys_grad, values_grad)
        )
    return dq.reshape(rows, heads, width), keys_grad, values_grad


def solution(mesh):
    in_specs = (
        P("seq", "head", None),
        P(("seq", "head"), None),
        P(("seq", "head"), None),
        P("seq", "head", None),
        P("seq", "head", None),
        P("seq", "head"),
        P(("seq", "head")),
    )
    out_specs = (P("seq", "head", None), P(("seq", "head"), None), P(("seq", "head"), None))
    return jax.shard_map(
        on_device, mesh=mesh, in_specs=in_specs, out_specs=out_specs, check_vma=False
    )
```

```python
import functools
import math

import jax
import jax.numpy as jnp
from jax import lax
from jax.experimental import pallas as pl
from jax.experimental.pallas import tpu as pltpu
from jax.sharding import PartitionSpec as P


WIN = 2048
TILE = 256
LOG2E = math.log2(math.e)
LN2 = math.log(2.0)
MASKED = -1e30
NN = (((1,), (0,)), ((), ()))
NT = (((1,), (1,)), ((), ()))
F32 = jnp.float32
BF16 = jnp.bfloat16


def shifted(value, axis, steps):
    count = lax.axis_size(axis)
    leading, last = (max(0, -steps), min(count, count - steps))
    return lax.ppermute(value, axis, [(source, source + steps) for source in range(leading, last)])


def swapped(value, axis):
    count = lax.axis_size(axis)
    return lax.ppermute(value, axis, [(source, source ^ 1) for source in range(count)])


def dot(a, b, dims):
    return lax.dot_general(a, b, dims, preferred_element_type=F32)


def halves(x):
    high = x.astype(BF16)
    return high, (x - high.astype(F32)).astype(BF16)


def kernel(blocks, sources, steps, rows, has_sum, *refs):
    operands = 1 + max(max(s) if isinstance(s, tuple) else s for s in sources)
    q_ref, g_ref, vec_ref, *rest = refs
    slabs, rest = rest[:operands], rest[operands:]
    sum_ref, rest = (rest[0], rest[1:]) if has_sum else (None, rest)
    dq_ref, rest = rest[0], rest[1:]
    outs, rest = rest[: len(sources)], rest[len(sources) :]
    k_hi, k_lo, kt_hi, kt_lo, v_hi, v_lo, dk_acc, dv_acc, first_ref = rest
    step = pl.program_id(0)
    width = q_ref.shape[1]

    @pl.when(step == 0)
    def _():
        dk_acc[...] = jnp.zeros_like(dk_acc)
        dv_acc[...] = jnp.zeros_like(dv_acc)
        odd = vec_ref[6:7, 0:1] > 0.5

        def part(source, at):
            if isinstance(source, tuple):
                return jnp.where(odd, slabs[source[1]][at, :], slabs[source[0]][at, :])
            return slabs[source][at, :]

        for s, source in enumerate(sources):
            at = pl.ds(s * rows, rows)
            keys, values = part(source, pl.ds(0, rows)), part(source, pl.ds(rows, rows))
            k_hi[at, :], k_lo[at, :] = halves(keys)
            kt_hi[:, at], kt_lo[:, at] = halves(keys.T)
            v_hi[at, :], v_lo[at, :] = halves(values)
            ids = part(source, pl.ds(2 * rows, slabs[0].shape[0] - 2 * rows))
            same = jnp.where(ids == vec_ref[5:6, 0:1], F32(1), F32(0))
            count = jnp.sum(jnp.sum(same, axis=0, keepdims=True), axis=1, keepdims=True)
            first_ref[s : s + 1, :] = jnp.broadcast_to(rows - count, (1, TILE))

    ready = {}

    def load(tile):
        if tile not in ready:
            at = pl.ds(tile * TILE, TILE)
            ready[tile] = (
                *halves(q_ref[at, :] * F32(LOG2E / math.sqrt(width))),
                *halves(g_ref[at, :]),
                vec_ref[:, at],
            )
        return ready[tile]

    def span(tile, block):
        start, size, _ = block
        if callable(start):
            start = pl.multiple_of(start(step * steps + tile), 128)
        return pl.ds(start, size), start

    def front(tile, block):
        q_hi, q_lo, g_hi, g_lo, _ = load(tile)
        at, _ = span(tile, block)
        scores = dot(k_hi[at, :], q_hi, NT) + dot(k_lo[at, :], q_hi, NT) + dot(k_hi[at, :], q_lo, NT)
        grad_probs = dot(v_hi[at, :], g_hi, NT) + dot(v_lo[at, :], g_hi, NT) + dot(v_hi[at, :], g_lo, NT)
        return scores, grad_probs

    totals = {}

    def back(tile, block, scores, grad_probs):
        q_hi, q_lo, g_hi, g_lo, vec = load(tile)
        at, start = span(tile, block)
        size, both = block[1], block[2]
        row = lax.broadcasted_iota(jnp.int32, (size, TILE), 0).astype(F32)
        if both:
            base = lax.convert_element_type(start, F32)
            low = jnp.maximum(vec[2:3, :], first_ref[0:1, :]) - base
            allowed = (row >= low) & (row <= vec[4:5, :] - base)
        else:
            allowed = row >= jnp.maximum(vec[3:4, :], first_ref[start // rows : start // rows + 1, :])
        probs = jnp.exp2(jnp.where(allowed, scores - vec[0:1, :], F32(MASKED)))
        grad_scores = probs * (grad_probs - vec[1:2, :])
        p_hi, p_lo = halves(probs)
        s_hi, s_lo = halves(grad_scores)
        dv_acc[at, :] += dot(p_hi, g_hi, NN) + dot(p_lo, g_hi, NN) + dot(p_hi, g_lo, NN)
        dk_acc[at, :] += dot(s_hi, q_hi, NN) + dot(s_lo, q_hi, NN) + dot(s_hi, q_lo, NN)
        new = dot(kt_hi[:, at], s_hi, NN) + dot(kt_lo[:, at], s_hi, NN) + dot(kt_hi[:, at], s_lo, NN)
        totals[tile] = totals[tile] + new if tile in totals else new

    work = [(tile, n) for tile in range(steps) for n in range(len(blocks))]
    coming = front(work[0][0], blocks[work[0][1]])
    for order, (tile, n) in enumerate(work):
        here = coming
        if order + 1 < len(work):
            coming = front(work[order + 1][0], blocks[work[order + 1][1]])
        back(tile, blocks[n], *here)
        if n + 1 == len(blocks):
            at = pl.ds(tile * TILE, TILE)
            dq = totals[tile].T * F32(1 / math.sqrt(width))
            dq_ref[at, :] = dq if sum_ref is None else dq + sum_ref[at, :]

    @pl.when(step == pl.num_programs(0) - 1)
    def _():
        for s, out in enumerate(outs):
            at = pl.ds(s * rows, rows)
            out[0:rows, :] = dk_acc[at, :] * F32(LN2)
            out[rows : 2 * rows, :] = dv_acc[at, :]


def attend(blocks, sources, q, g, vec, slabs, rows, dq_sum):
    total, width = q.shape
    count = len(sources)
    keys = count * rows
    tiles = total // TILE
    steps = math.gcd(tiles, 4)
    tile_spec = pl.BlockSpec((steps * TILE, width), lambda i: (i, 0))
    whole = lambda shape: pl.BlockSpec(shape, lambda i: (0, 0))
    sums = [] if dq_sum is None else [dq_sum]
    computed = sum(b[1] for b in blocks)
    results = pl.pallas_call(
        functools.partial(kernel, blocks, sources, steps, rows, bool(sums)),
        grid=(tiles // steps,),
        in_specs=[tile_spec, tile_spec, pl.BlockSpec((8, steps * TILE), lambda i: (0, i))]
        + [whole(slabs[0].shape)] * len(slabs)
        + [tile_spec] * len(sums),
        out_specs=[tile_spec] + [whole((2 * rows, width))] * count,
        out_shape=[jax.ShapeDtypeStruct((total, width), F32)]
        + [jax.ShapeDtypeStruct((2 * rows, width), F32)] * count,
        scratch_shapes=[
            pltpu.VMEM((keys, width), BF16),
            pltpu.VMEM((keys, width), BF16),
            pltpu.VMEM((width, keys), BF16),
            pltpu.VMEM((width, keys), BF16),
            pltpu.VMEM((keys, width), BF16),
            pltpu.VMEM((keys, width), BF16),
            pltpu.VMEM((keys, width), F32),
            pltpu.VMEM((keys, width), F32),
            pltpu.VMEM((8, TILE), F32),
        ],
        compiler_params=pltpu.CompilerParams(vmem_limit_bytes=63 * 1024 * 1024),
        cost_estimate=pl.CostEstimate(
            flops=30 * total * computed * width, bytes_accessed=12 * total * width, transcendentals=total * computed
        ),
    )(q, g, vec, *slabs, *sums)
    return results[0], results[1:]


def program(queries, key_rows, value_rows, forward_out, out_grad, log_norm, doc_ids):
    rows, heads, width = queries.shape
    reach = WIN // rows
    ids = doc_ids.astype(F32) + 1.0
    if lax.axis_size("head") > 1:
        gather = functools.partial(lax.all_gather, axis_name="head", axis=0, tiled=True)
        key_rows, value_rows, ids = gather(key_rows), gather(value_rows), gather(ids)
    id_rows = 8 * pl.cdiv(rows, 8 * width)
    id_part = jnp.pad(ids, (0, id_rows * width - rows)).reshape(id_rows, width)
    own = jnp.concatenate([key_rows, value_rows, id_part], axis=0)
    odd = lax.axis_index("seq") % 2 == 1

    mine, other = {0: own}, {}
    for distance in range(reach, 0, -2):
        mine[distance] = shifted(own, "seq", distance)
    for distance in range(reach, -1, -2):
        other[distance] = swapped(mine[distance], "seq")

    token = jnp.arange(rows, dtype=F32)
    before = jnp.sum((ids[None, :] < ids[:, None]).astype(F32), axis=1)
    first = before == 0
    per_token = jnp.stack(
        [
            jnp.where(first, token + 1, rows + before),
            jnp.where(first, 0.0, 1e9),
            token + rows,
            jnp.broadcast_to(ids[0], (rows,)),
            jnp.broadcast_to(odd.astype(F32), (rows,)),
        ]
    )
    spread = jnp.broadcast_to(per_token[:, :, None], (5, rows, heads)).reshape(5, rows * heads)
    delta = jnp.sum(out_grad * forward_out, axis=-1).reshape(1, -1)
    scaled = (log_norm * F32(LOG2E)).reshape(1, -1)
    vec = jnp.concatenate([scaled, delta, spread, jnp.zeros((1, rows * heads), F32)], axis=0)

    q = queries.reshape(rows * heads, width)
    g = out_grad.reshape(rows * heads, width)
    tokens = TILE // heads
    edge = max(tokens, 128)
    edges = ((lambda i: (i * tokens) // edge * edge, rows + edge, True), (2 * rows, rows, False))
    dq, (far, own_part, cross) = attend(
        edges, (0, 1, (2, 3)), q, g, vec, [mine[reach], own, other[reach], other[0]], rows, None
    )
    cross = swapped(cross, "seq")
    far = far + jnp.where(odd, cross, 0.0)
    own_part = own_part + jnp.where(odd, 0.0, cross)
    returned = [shifted(far, "seq", -reach)]
    rest = list(range(reach - 2, 0, -2))
    groups = [rest[:-1], rest[-1:]] if len(rest) > 1 else [rest]
    for group in groups:
        slabs = [x for d in group for x in (mine[d], other[d])]
        blocks = tuple((s * rows, rows, False) for s in range(len(slabs)))
        dq, parts = attend(blocks, tuple(range(len(slabs))), q, g, vec, slabs, rows, dq)
        for s, d in enumerate(group):
            handed = swapped(parts[2 * s + 1], "seq")
            joined = parts[2 * s] + handed
            returned.append(shifted(joined, "seq", -d))
    for part in returned:
        own_part = own_part + part
    keys_grad, values_grad = own_part[:rows], own_part[rows:]
    if lax.axis_size("head") > 1:
        keys_grad, values_grad = (
            lax.psum_scatter(x, "head", scatter_dimension=0, tiled=True) for x in (keys_grad, values_grad)
        )
    return dq.reshape(rows, heads, width), keys_grad, values_grad


def solution(mesh):
    in_specs = (
        P("seq", "head", None),
        P(("seq", "head"), None),
        P(("seq", "head"), None),
        P("seq", "head", None),
        P("seq", "head", None),
        P("seq", "head"),
        P(("seq", "head")),
    )
    out_specs = (P("seq", "head", None), P(("seq", "head"), None), P(("seq", "head"), None))
    return jax.shard_map(program, mesh=mesh, in_specs=in_specs, out_specs=out_specs, check_vma=False)
```

```python
import functools
import math

import jax
import jax.numpy as jnp
from jax import lax
from jax.experimental import pallas as pl
from jax.experimental.pallas import tpu as pltpu
from jax.sharding import PartitionSpec as P


WIN = 2048
TILE = 256
LOG2E = math.log2(math.e)
LN2 = math.log(2.0)
MASKED = -1e30
NN = (((1,), (0,)), ((), ()))
NT = (((1,), (1,)), ((), ()))
F32 = jnp.float32
BF16 = jnp.bfloat16


def shifted(value, axis, steps):
    count = lax.axis_size(axis)
    leading, last = (max(0, -steps), min(count, count - steps))
    return lax.ppermute(value, axis, [(source, source + steps) for source in range(leading, last)])


def swapped(value, axis):
    count = lax.axis_size(axis)
    return lax.ppermute(value, axis, [(source, source ^ 1) for source in range(count)])


def dot(a, b, dims):
    return lax.dot_general(a, b, dims, preferred_element_type=F32)


def halves(x):
    high = x.astype(BF16)
    return high, (x - high.astype(F32)).astype(BF16)


def pack(k_ref, v_ref, ids_ref, out_ref):
    rows = k_ref.shape[0]
    out_ref[0:rows, :] = k_ref[...]
    out_ref[rows : 2 * rows, :] = v_ref[...]
    out_ref[2 * rows :, :] = jnp.zeros_like(out_ref[2 * rows :, :])
    out_ref[2 * rows : 2 * rows + ids_ref.shape[0], :] = ids_ref[...].astype(F32) + F32(1)


def packed(keys, values, ids):
    rows, width = keys.shape
    lines = pl.cdiv(rows, width)
    lined = jnp.pad(ids, (0, lines * width - rows), constant_values=-1).reshape(lines, width)
    return pl.pallas_call(
        pack, out_shape=jax.ShapeDtypeStruct((2 * rows + 8 * pl.cdiv(lines, 8), width), F32)
    )(keys, values, lined)


def kernel(blocks, sources, steps, rows, opens, *refs):
    operands = 1 + max(max(s) if isinstance(s, tuple) else s for s in sources)
    q_ref, g_ref, vec_ref, *rest = refs
    slabs, rest = rest[:operands], rest[operands:]
    side_ref, rest = rest[0], rest[1:]
    delta_ref = None
    if not opens:
        delta_ref, rest = rest[0], rest[1:]
    dq_ref, rest = rest[0], rest[1:]
    if opens:
        delta_ref, rest = rest[0], rest[1:]
    outs, rest = rest[: len(sources)], rest[len(sources) :]
    k_hi, k_lo, kt_hi, kt_lo, v_hi, v_lo, dk_acc, dv_acc, first_ref = rest
    step = pl.program_id(0)
    width = q_ref.shape[1]

    @pl.when(step == 0)
    def _():
        dk_acc[...] = jnp.zeros_like(dk_acc)
        dv_acc[...] = jnp.zeros_like(dv_acc)
        odd = vec_ref[6:7, 0:1] > 0.5

        def part(source, at):
            if isinstance(source, tuple):
                return jnp.where(odd, slabs[source[1]][at, :], slabs[source[0]][at, :])
            return slabs[source][at, :]

        for s, source in enumerate(sources):
            at = pl.ds(s * rows, rows)
            keys, values = part(source, pl.ds(0, rows)), part(source, pl.ds(rows, rows))
            k_hi[at, :], k_lo[at, :] = halves(keys)
            kt_hi[:, at], kt_lo[:, at] = halves(keys.T)
            v_hi[at, :], v_lo[at, :] = halves(values)
            ids = part(source, pl.ds(2 * rows, slabs[0].shape[0] - 2 * rows))
            same = jnp.where(ids == vec_ref[5:6, 0:1], F32(1), F32(0))
            count = jnp.sum(jnp.sum(same, axis=0, keepdims=True), axis=1, keepdims=True)
            first_ref[s : s + 1, :] = jnp.broadcast_to(rows - count, (1, TILE))

    ready = {}

    def load(tile):
        if tile not in ready:
            at = pl.ds(tile * TILE, TILE)
            ready[tile] = (
                *halves(q_ref[at, :] * F32(LOG2E / math.sqrt(width))),
                *halves(g_ref[at, :]),
                vec_ref[:, at],
            )
            if opens:
                high, low = halves(g_ref[at, :] * side_ref[at, :])
                ones = jnp.ones((16, width), BF16)
                delta_ref[:, at] = (dot(ones, high, NT) + dot(ones, low, NT))[0:8, :]
        return ready[tile]

    def span(tile, block):
        start, size, _ = block
        if callable(start):
            start = pl.multiple_of(start(step * steps + tile), 128)
        return pl.ds(start, size), start

    def front(tile, block):
        q_hi, q_lo, g_hi, g_lo, _ = load(tile)
        at, _ = span(tile, block)
        scores = dot(k_hi[at, :], q_hi, NT) + dot(k_lo[at, :], q_hi, NT) + dot(k_hi[at, :], q_lo, NT)
        grad_probs = dot(v_hi[at, :], g_hi, NT) + dot(v_lo[at, :], g_hi, NT) + dot(v_hi[at, :], g_lo, NT)
        return scores, grad_probs

    totals = {}

    def back(tile, block, scores, grad_probs):
        q_hi, q_lo, g_hi, g_lo, vec = load(tile)
        at, start = span(tile, block)
        size, both = block[1], block[2]
        row = lax.broadcasted_iota(jnp.int32, (size, TILE), 0).astype(F32)
        if both:
            base = lax.convert_element_type(start, F32)
            low = jnp.maximum(vec[2:3, :], first_ref[0:1, :]) - base
            allowed = (row >= low) & (row <= vec[4:5, :] - base)
        else:
            allowed = row >= jnp.maximum(vec[3:4, :], first_ref[start // rows : start // rows + 1, :])
        probs = jnp.exp2(jnp.where(allowed, scores - vec[0:1, :], F32(MASKED)))
        grad_scores = probs * (grad_probs - delta_ref[0:1, pl.ds(tile * TILE, TILE)])
        p_hi, p_lo = halves(probs)
        s_hi, s_lo = halves(grad_scores)
        dv_acc[at, :] += dot(p_hi, g_hi, NN) + dot(p_lo, g_hi, NN) + dot(p_hi, g_lo, NN)
        dk_acc[at, :] += dot(s_hi, q_hi, NN) + dot(s_lo, q_hi, NN) + dot(s_hi, q_lo, NN)
        new = dot(kt_hi[:, at], s_hi, NN) + dot(kt_lo[:, at], s_hi, NN) + dot(kt_hi[:, at], s_lo, NN)
        totals[tile] = totals[tile] + new if tile in totals else new

    work = [(tile, n) for tile in range(steps) for n in range(len(blocks))]
    coming = front(work[0][0], blocks[work[0][1]])
    for order, (tile, n) in enumerate(work):
        here = coming
        if order + 1 < len(work):
            coming = front(work[order + 1][0], blocks[work[order + 1][1]])
        back(tile, blocks[n], *here)
        if n + 1 == len(blocks):
            at = pl.ds(tile * TILE, TILE)
            dq = totals[tile].T * F32(1 / math.sqrt(width))
            dq_ref[at, :] = dq if opens else dq + side_ref[at, :]

    @pl.when(step == pl.num_programs(0) - 1)
    def _():
        for s, out in enumerate(outs):
            at = pl.ds(s * rows, rows)
            out[0:rows, :] = dk_acc[at, :] * F32(LN2)
            out[rows : 2 * rows, :] = dv_acc[at, :]


def attend(blocks, sources, q, g, vec, slabs, rows, side, delta=None):
    total, width = q.shape
    count = len(sources)
    keys = count * rows
    tiles = total // TILE
    steps = math.gcd(tiles, 4)
    tile_spec = pl.BlockSpec((steps * TILE, width), lambda i: (i, 0))
    whole = lambda shape: pl.BlockSpec(shape, lambda i: (0, 0))
    opens = delta is None
    lane_spec = pl.BlockSpec((8, steps * TILE), lambda i: (0, i))
    computed = sum(b[1] for b in blocks)
    results = pl.pallas_call(
        functools.partial(kernel, blocks, sources, steps, rows, opens),
        grid=(tiles // steps,),
        in_specs=[tile_spec, tile_spec, lane_spec]
        + [whole(slabs[0].shape)] * len(slabs)
        + [tile_spec]
        + ([] if opens else [lane_spec]),
        out_specs=[tile_spec] + ([lane_spec] if opens else []) + [whole((2 * rows, width))] * count,
        out_shape=[jax.ShapeDtypeStruct((total, width), F32)]
        + ([jax.ShapeDtypeStruct((8, total), F32)] if opens else [])
        + [jax.ShapeDtypeStruct((2 * rows, width), F32)] * count,
        scratch_shapes=[
            pltpu.VMEM((keys, width), BF16),
            pltpu.VMEM((keys, width), BF16),
            pltpu.VMEM((width, keys), BF16),
            pltpu.VMEM((width, keys), BF16),
            pltpu.VMEM((keys, width), BF16),
            pltpu.VMEM((keys, width), BF16),
            pltpu.VMEM((keys, width), F32),
            pltpu.VMEM((keys, width), F32),
            pltpu.VMEM((8, TILE), F32),
        ],
        compiler_params=pltpu.CompilerParams(vmem_limit_bytes=24 * 1024 * 1024),
        cost_estimate=pl.CostEstimate(
            flops=30 * total * computed * width, bytes_accessed=12 * total * width, transcendentals=total * computed
        ),
    )(q, g, vec, *slabs, side, *([] if opens else [delta]))
    return results


def program(queries, key_rows, value_rows, forward_out, out_grad, log_norm, doc_ids):
    rows, heads, width = queries.shape
    reach = WIN // rows
    ids = doc_ids
    if lax.axis_size("head") > 1:
        gather = functools.partial(lax.all_gather, axis_name="head", axis=0, tiled=True)
        key_rows, value_rows = gather(key_rows), gather(value_rows)
        ids = gather(ids.astype(F32)).astype(jnp.int32)
    own = packed(key_rows, value_rows, ids)
    odd = lax.axis_index("seq") % 2 == 1

    mine, other = {0: own}, {}
    for distance in range(reach, 0, -2):
        mine[distance] = shifted(own, "seq", distance)
    for distance in range(reach, -1, -2):
        other[distance] = swapped(mine[distance], "seq")

    token = jnp.arange(rows, dtype=F32)
    before = jnp.sum((ids[None, :] < ids[:, None]).astype(F32), axis=1)
    first = before == 0
    per_token = jnp.stack(
        [
            jnp.where(first, token + 1, rows + before),
            jnp.where(first, 0.0, 1e9),
            token + rows,
            jnp.broadcast_to(ids[0].astype(F32) + 1, (rows,)),
            jnp.broadcast_to(odd.astype(F32), (rows,)),
        ]
    )
    spread = jnp.broadcast_to(per_token[:, :, None], (5, rows, heads)).reshape(5, rows * heads)
    scaled = (log_norm * F32(LOG2E)).reshape(1, -1)
    blank = jnp.zeros((1, rows * heads), F32)
    vec = jnp.concatenate([scaled, blank, spread, blank], axis=0)

    q = queries.reshape(rows * heads, width)
    g = out_grad.reshape(rows * heads, width)
    tokens = TILE // heads
    edge = max(tokens, 128)
    edges = ((lambda i: (i * tokens) // edge * edge, rows + edge, True), (2 * rows, rows, False))
    out = forward_out.reshape(rows * heads, width)
    here = lambda x: pltpu.with_memory_space_constraint(x, pltpu.HBM)
    dq, delta, far, own_part, cross = attend(
        edges, (0, 1, (2, 3)), here(q), here(g), vec, [mine[reach], own, other[reach], other[0]], rows, here(out)
    )
    cross = swapped(cross, "seq")
    returned = [shifted(far + jnp.where(odd, cross, 0.0), "seq", -reach)]
    returned.append(jnp.where(odd, 0.0, cross))
    blocks = ((0, rows, False), (rows, rows, False))
    for d in range(reach - 2, 0, -2):
        dq, part, hand = attend(blocks, (0, 1), q, g, vec, [mine[d], other[d]], rows, dq, delta)
        hand = swapped(hand, "seq")
        returned.append(shifted(part + hand, "seq", -d))
    keys_grad = sum([part[:rows] for part in returned], own_part[:rows])
    values_grad = sum([part[rows:] for part in returned], own_part[rows:])
    if lax.axis_size("head") > 1:
        keys_grad, values_grad = (
            lax.psum_scatter(x, "head", scatter_dimension=0, tiled=True) for x in (keys_grad, values_grad)
        )
    return dq.reshape(rows, heads, width), keys_grad, values_grad


def solution(mesh):
    in_specs = (
        P("seq", "head", None),
        P(("seq", "head"), None),
        P(("seq", "head"), None),
        P("seq", "head", None),
        P("seq", "head", None),
        P("seq", "head"),
        P(("seq", "head")),
    )
    out_specs = (P("seq", "head", None), P(("seq", "head"), None), P(("seq", "head"), None))
    return jax.shard_map(program, mesh=mesh, in_specs=in_specs, out_specs=out_specs, check_vma=False)
```

```python
import functools
import math

import jax
import jax.numpy as jnp
from jax import lax
from jax.experimental import pallas as pl
from jax.experimental.pallas import tpu as pltpu
from jax.sharding import PartitionSpec as P


WIN = 2048
TILE = 256
LOG2E = math.log2(math.e)
KEPT = 2
GRANT = 24 * 1024 * 1024
LN2 = math.log(2.0)
MASKED = -1e30
NN = (((1,), (0,)), ((), ()))
NT = (((1,), (1,)), ((), ()))
F32 = jnp.float32
BF16 = jnp.bfloat16


def shifted(value, axis, steps):
    count = lax.axis_size(axis)
    leading, last = (max(0, -steps), min(count, count - steps))
    return lax.ppermute(value, axis, [(source, source + steps) for source in range(leading, last)])


def swapped(value, axis):
    count = lax.axis_size(axis)
    return lax.ppermute(value, axis, [(source, source ^ 1) for source in range(count)])


def dot(a, b, dims):
    return lax.dot_general(a, b, dims, preferred_element_type=F32)


def halves(x):
    high = x.astype(BF16)
    return high, (x - high.astype(F32)).astype(BF16)


def pack(k_ref, v_ref, ids_ref, out_ref):
    rows = k_ref.shape[0]
    out_ref[0:rows, :] = k_ref[...]
    out_ref[rows : 2 * rows, :] = v_ref[...]
    out_ref[2 * rows :, :] = jnp.zeros_like(out_ref[2 * rows :, :])
    out_ref[2 * rows : 2 * rows + ids_ref.shape[0], :] = ids_ref[...].astype(F32) + F32(1)


def packed(keys, values, ids):
    rows, width = keys.shape
    lines = pl.cdiv(rows, width)
    lined = jnp.pad(ids, (0, lines * width - rows), constant_values=-1).reshape(lines, width)
    return pl.pallas_call(
        pack, out_shape=jax.ShapeDtypeStruct((2 * rows + 8 * pl.cdiv(lines, 8), width), F32)
    )(keys, values, lined)


def kernel(blocks, sources, steps, rows, opens, keeps, *refs):
    operands = 1 + max(max(s) if isinstance(s, tuple) else s for s in sources)
    q_ref, g_ref, vec_ref, *rest = refs
    slabs, rest = rest[:operands], rest[operands:]
    if opens:
        out_ref, dq_ref, delta_ref, *rest = rest
    elif keeps:
        delta_ref, keep_hi, keep_lo, *rest = rest
    else:
        delta_ref, sum_ref, dq_ref, *rest = rest
    outs, rest = rest[: len(sources)], rest[len(sources) :]
    k_hi, k_lo, kt_hi, kt_lo, v_hi, v_lo, dk_acc, dv_acc, first_ref = rest
    step = pl.program_id(0)
    width = q_ref.shape[1]

    @pl.when(step == 0)
    def _():
        dk_acc[...] = jnp.zeros_like(dk_acc)
        dv_acc[...] = jnp.zeros_like(dv_acc)
        odd = vec_ref[6:7, 0:1] > 0.5

        def part(source, at):
            if isinstance(source, tuple):
                return jnp.where(odd, slabs[source[1]][at, :], slabs[source[0]][at, :])
            return slabs[source][at, :]

        for s, source in enumerate(sources):
            at = pl.ds(s * rows, rows)
            keys, values = part(source, pl.ds(0, rows)), part(source, pl.ds(rows, rows))
            k_hi[at, :], k_lo[at, :] = halves(keys)
            if not keeps:
                kt_hi[:, at], kt_lo[:, at] = halves(keys.T)
            v_hi[at, :], v_lo[at, :] = halves(values)
            ids = part(source, pl.ds(2 * rows, slabs[0].shape[0] - 2 * rows))
            same = jnp.where(ids == vec_ref[5:6, 0:1], F32(1), F32(0))
            count = jnp.sum(jnp.sum(same, axis=0, keepdims=True), axis=1, keepdims=True)
            first_ref[s : s + 1, :] = jnp.broadcast_to(rows - count, (1, TILE))

    ready = {}

    def load(tile):
        if tile not in ready:
            at = pl.ds(tile * TILE, TILE)
            ready[tile] = (
                *halves(q_ref[at, :] * F32(LOG2E / math.sqrt(width))),
                *halves(g_ref[at, :]),
                vec_ref[:, at],
            )
            if opens:
                high, low = halves(g_ref[at, :] * out_ref[at, :])
                ones = jnp.ones((16, width), BF16)
                delta_ref[:, at] = (dot(ones, high, NT) + dot(ones, low, NT))[0:8, :]
        return ready[tile]

    def span(tile, block):
        start, size, _ = block
        if callable(start):
            start = pl.multiple_of(start(step * steps + tile), 128)
        return pl.ds(start, size), start

    def front(tile, block):
        q_hi, q_lo, g_hi, g_lo, _ = load(tile)
        at, _ = span(tile, block)
        scores = dot(k_hi[at, :], q_hi, NT) + dot(k_lo[at, :], q_hi, NT) + dot(k_hi[at, :], q_lo, NT)
        grad_probs = dot(v_hi[at, :], g_hi, NT) + dot(v_lo[at, :], g_hi, NT) + dot(v_hi[at, :], g_lo, NT)
        return scores, grad_probs

    totals = {}

    def back(tile, block, scores, grad_probs):
        q_hi, q_lo, g_hi, g_lo, vec = load(tile)
        at, start = span(tile, block)
        size, both = block[1], block[2]
        row = lax.broadcasted_iota(jnp.int32, (size, TILE), 0).astype(F32)
        if both:
            base = lax.convert_element_type(start, F32)
            low = jnp.maximum(vec[2:3, :], first_ref[0:1, :]) - base
            allowed = (row >= low) & (row <= vec[4:5, :] - base)
        else:
            allowed = row >= jnp.maximum(vec[3:4, :], first_ref[start // rows : start // rows + 1, :])
        probs = jnp.exp2(jnp.where(allowed, scores - vec[0:1, :], F32(MASKED)))
        grad_scores = probs * (grad_probs - delta_ref[0:1, pl.ds(tile * TILE, TILE)])
        p_hi, p_lo = halves(probs)
        s_hi, s_lo = halves(grad_scores)
        dv_acc[at, :] += dot(p_hi, g_hi, NN) + dot(p_lo, g_hi, NN) + dot(p_hi, g_lo, NN)
        dk_acc[at, :] += dot(s_hi, q_hi, NN) + dot(s_lo, q_hi, NN) + dot(s_hi, q_lo, NN)
        if keeps:
            across = pl.ds(tile * TILE, TILE)
            keep_hi[at, across], keep_lo[at, across] = s_hi, s_lo
            return
        new = dot(kt_hi[:, at], s_hi, NN) + dot(kt_lo[:, at], s_hi, NN) + dot(kt_hi[:, at], s_lo, NN)
        totals[tile] = totals[tile] + new if tile in totals else new

    work = [(tile, n) for tile in range(steps) for n in range(len(blocks))]
    coming = front(work[0][0], blocks[work[0][1]])
    for order, (tile, n) in enumerate(work):
        here = coming
        if order + 1 < len(work):
            coming = front(work[order + 1][0], blocks[work[order + 1][1]])
        back(tile, blocks[n], *here)
        if not keeps and n + 1 == len(blocks):
            at = pl.ds(tile * TILE, TILE)
            dq = totals[tile].T * F32(1 / math.sqrt(width))
            dq_ref[at, :] = dq if opens else sum_ref[at, :] + dq

    @pl.when(step == pl.num_programs(0) - 1)
    def _():
        for s, out in enumerate(outs):
            at = pl.ds(s * rows, rows)
            out[0:rows, :] = dk_acc[at, :] * F32(LN2)
            out[rows : 2 * rows, :] = dv_acc[at, :]


def attend(blocks, sources, q, g, vec, slabs, rows, *side):
    total, width = q.shape
    count = len(sources)
    keys = count * rows
    tiles = total // TILE
    steps = math.gcd(tiles, 4)
    opens, keeps = side[0].shape[0] == total, len(side) == 1 and side[0].shape[0] != total
    tile_spec = pl.BlockSpec((steps * TILE, width), lambda i: (i, 0))
    lane_spec = pl.BlockSpec((8, steps * TILE), lambda i: (0, i))
    keep_spec = pl.BlockSpec((keys, steps * TILE), lambda i: (0, i))
    whole = lambda shape: pl.BlockSpec(shape, lambda i: (0, 0))
    computed = sum(b[1] for b in blocks)
    taken, given = [tile_spec], [tile_spec]
    shapes = [jax.ShapeDtypeStruct((total, width), F32)]
    if opens:
        given = [tile_spec, lane_spec]
        shapes.append(jax.ShapeDtypeStruct((8, total), F32))
    elif keeps:
        taken, given = [lane_spec], [keep_spec] * 2
        shapes = [pltpu.HBM((keys, total), BF16)] * 2
    else:
        taken = [lane_spec, tile_spec]
    return pl.pallas_call(
        functools.partial(kernel, blocks, sources, steps, rows, opens, keeps),
        grid=(tiles // steps,),
        in_specs=[tile_spec, tile_spec, lane_spec]
        + [whole(slabs[0].shape)] * len(slabs)
        + taken,
        out_specs=given + [whole((2 * rows, width))] * count,
        out_shape=shapes + [jax.ShapeDtypeStruct((2 * rows, width), F32)] * count,
        scratch_shapes=[
            pltpu.VMEM((keys, width), BF16),
            pltpu.VMEM((keys, width), BF16),
            pltpu.VMEM((width, keys), BF16),
            pltpu.VMEM((width, keys), BF16),
            pltpu.VMEM((keys, width), BF16),
            pltpu.VMEM((keys, width), BF16),
            pltpu.VMEM((keys, width), F32),
            pltpu.VMEM((keys, width), F32),
            pltpu.VMEM((8, TILE), F32),
        ],
        compiler_params=pltpu.CompilerParams(vmem_limit_bytes=GRANT),
        cost_estimate=pl.CostEstimate(
            flops=30 * total * computed * width, bytes_accessed=12 * total * width, transcendentals=total * computed
        ),
    )(q, g, vec, *slabs, *side)


def close(steps, count, rows, *refs):
    part_ref, refs = refs[0], refs[1:]
    kept, slabs, dq_ref, kt_hi, kt_lo = refs[:count], refs[count : 2 * count], refs[-3], refs[-2], refs[-1]
    width = part_ref.shape[1]

    @pl.when(pl.program_id(0) == 0)
    def _():
        for s, slab in enumerate(slabs):
            at = pl.ds(s * rows, rows)
            kt_hi[:, at], kt_lo[:, at] = halves(slab[...].T)

    for tile in range(steps):
        at = pl.ds(tile * TILE, TILE)
        total = None
        for n in range(0, count, 2):
            keys = pl.ds(n * rows, 2 * rows)
            high, low = kept[n][:, at], kept[n + 1][:, at]
            new = dot(kt_hi[:, keys], high, NN) + dot(kt_lo[:, keys], high, NN) + dot(kt_hi[:, keys], low, NN)
            total = new if total is None else total + new
        dq_ref[at, :] = part_ref[at, :] + total.T * F32(1 / math.sqrt(width))


def query_grads(part, kept, slabs, rows):
    total, width = part.shape
    tiles = total // TILE
    steps = math.gcd(tiles, 2)
    count = len(slabs)
    tile_spec = pl.BlockSpec((steps * TILE, width), lambda i: (i, 0))
    return pl.pallas_call(
        functools.partial(close, steps, count, rows),
        grid=(tiles // steps,),
        in_specs=[tile_spec]
        + [pl.BlockSpec((2 * rows, steps * TILE), lambda i: (0, i))] * count
        + [pl.BlockSpec((rows, width), lambda i: (0, 0))] * count,
        out_specs=tile_spec,
        out_shape=jax.ShapeDtypeStruct((total, width), F32),
        scratch_shapes=[pltpu.VMEM((width, count * rows), BF16)] * 2,
        compiler_params=pltpu.CompilerParams(vmem_limit_bytes=GRANT),
        cost_estimate=pl.CostEstimate(
            flops=6 * total * count * rows * width, bytes_accessed=4 * total * (count * rows + 2 * width), transcendentals=0
        ),
    )(part, *kept, *slabs)


def program(queries, key_rows, value_rows, forward_out, out_grad, log_norm, doc_ids):
    rows, heads, width = queries.shape
    reach = WIN // rows
    ids = doc_ids
    if lax.axis_size("head") > 1:
        gather = functools.partial(lax.all_gather, axis_name="head", axis=0, tiled=True)
        key_rows, value_rows = gather(key_rows), gather(value_rows)
        ids = gather(ids.astype(F32)).astype(jnp.int32)
    own = packed(key_rows, value_rows, ids)
    odd = lax.axis_index("seq") % 2 == 1

    mine, other = {0: own}, {}
    for distance in range(reach, 0, -2):
        mine[distance] = shifted(own, "seq", distance)
    for distance in range(reach, -1, -2):
        other[distance] = swapped(mine[distance], "seq")

    token = jnp.arange(rows, dtype=F32)
    before = jnp.sum((ids[None, :] < ids[:, None]).astype(F32), axis=1)
    first = before == 0
    per_token = jnp.stack(
        [
            jnp.where(first, token + 1, rows + before),
            jnp.where(first, 0.0, 1e9),
            token + rows,
            jnp.broadcast_to(ids[0].astype(F32) + 1, (rows,)),
            jnp.broadcast_to(odd.astype(F32), (rows,)),
        ]
    )
    spread = jnp.broadcast_to(per_token[:, :, None], (5, rows, heads)).reshape(5, rows * heads)
    scaled = (log_norm * F32(LOG2E)).reshape(1, -1)
    blank = jnp.zeros((1, rows * heads), F32)
    vec = jnp.concatenate([scaled, blank, spread, blank], axis=0)

    q = queries.reshape(rows * heads, width)
    g = out_grad.reshape(rows * heads, width)
    tokens = TILE // heads
    edge = max(tokens, 128)
    edges = ((lambda i: (i * tokens) // edge * edge, rows + edge, True), (2 * rows, rows, False))
    out = forward_out.reshape(rows * heads, width)
    here = lambda x: pltpu.with_memory_space_constraint(x, pltpu.HBM)
    dq, delta, far, own_part, cross = attend(
        edges, (0, 1, (2, 3)), here(q), here(g), vec, [mine[reach], own, other[reach], other[0]], rows, here(out)
    )
    cross = swapped(cross, "seq")
    returned = [shifted(far + jnp.where(odd, cross, 0.0), "seq", -reach)]
    returned.append(jnp.where(odd, 0.0, cross))
    blocks = ((0, rows, False), (rows, rows, False))
    kept, slabs = [], []
    for d in range(reach - 2, 0, -2):
        if d > KEPT:
            dq, part, hand = attend(blocks, (0, 1), q, g, vec, [mine[d], other[d]], rows, delta, dq)
        else:
            high, low, part, hand = attend(blocks, (0, 1), q, g, vec, [mine[d], other[d]], rows, delta)
            kept += [high, low]
            slabs += [mine[d], other[d]]
        hand = swapped(hand, "seq")
        returned.append(shifted(part + hand, "seq", -d))
    dq = query_grads(here(dq), [here(x) for x in kept], [here(x) for x in slabs], rows)
    keys_grad = sum([part[:rows] for part in returned], own_part[:rows])
    values_grad = sum([part[rows:] for part in returned], own_part[rows:])
    if lax.axis_size("head") > 1:
        keys_grad, values_grad = (
            lax.psum_scatter(x, "head", scatter_dimension=0, tiled=True) for x in (keys_grad, values_grad)
        )
    return dq.reshape(rows, heads, width), keys_grad, values_grad


def solution(mesh):
    in_specs = (
        P("seq", "head", None),
        P(("seq", "head"), None),
        P(("seq", "head"), None),
        P("seq", "head", None),
        P("seq", "head", None),
        P("seq", "head"),
        P(("seq", "head")),
    )
    out_specs = (P("seq", "head", None), P(("seq", "head"), None), P(("seq", "head"), None))
    return jax.shard_map(program, mesh=mesh, in_specs=in_specs, out_specs=out_specs, check_vma=False)
```

```python
import functools
import math

import jax
import jax.numpy as jnp
from jax import lax
from jax.experimental import pallas as pl
from jax.experimental.pallas import tpu as pltpu
from jax.sharding import PartitionSpec as P


WIN = 2048
TILE = 256
LANES = 128
LOG2E = math.log2(math.e)
KEPT = 4
GRANT = 24 * 1024 * 1024
LN2 = math.log(2.0)
MASKED = -1e30
NN = (((1,), (0,)), ((), ()))
NT = (((1,), (1,)), ((), ()))
F32 = jnp.float32
BF16 = jnp.bfloat16


def shifted(value, axis, steps):
    count = lax.axis_size(axis)
    leading, last = (max(0, -steps), min(count, count - steps))
    return lax.ppermute(value, axis, [(source, source + steps) for source in range(leading, last)])


def swapped(value, axis):
    count = lax.axis_size(axis)
    return lax.ppermute(value, axis, [(source, source ^ 1) for source in range(count)])


def dot(a, b, dims):
    return lax.dot_general(a, b, dims, preferred_element_type=F32)


def halves(x):
    high = x.astype(BF16)
    return high, (x - high.astype(F32)).astype(BF16)


def pack(k_ref, v_ref, ids_ref, out_ref):
    rows = k_ref.shape[0]
    out_ref[0:rows, :] = k_ref[...]
    out_ref[rows : 2 * rows, :] = v_ref[...]
    out_ref[2 * rows :, :] = jnp.zeros_like(out_ref[2 * rows :, :])
    out_ref[2 * rows : 2 * rows + ids_ref.shape[0], :] = ids_ref[...].astype(F32) + F32(1)


def packed(keys, values, ids):
    rows, width = keys.shape
    lines = pl.cdiv(rows, width)
    lined = jnp.pad(ids, (0, lines * width - rows), constant_values=-1).reshape(lines, width)
    return pl.pallas_call(
        pack, out_shape=jax.ShapeDtypeStruct((2 * rows + 8 * pl.cdiv(lines, 8), width), F32)
    )(keys, values, lined)


def kernel(blocks, sources, steps, rows, opens, keeps, *refs):
    operands = 1 + max(max(s) if isinstance(s, tuple) else s for s in sources)
    q_ref, g_ref, vec_ref, *rest = refs
    slabs, rest = rest[:operands], rest[operands:]
    if opens:
        out_ref, dq_ref, delta_ref, *rest = rest
    elif keeps:
        delta_ref, keep_hi, keep_lo, *rest = rest
    else:
        delta_ref, sum_ref, dq_ref, *rest = rest
    outs, rest = rest[: len(sources)], rest[len(sources) :]
    k_hi, k_lo, kt_hi, kt_lo, v_hi, v_lo, dk_acc, dv_acc, first_ref, *pads = rest
    step = pl.program_id(0)
    width = q_ref.shape[1]

    @pl.when(step == 0)
    def _():
        dk_acc[...] = jnp.zeros_like(dk_acc)
        dv_acc[...] = jnp.zeros_like(dv_acc)
        odd = vec_ref[6:7, 0:1] > 0.5

        def part(source, at):
            if isinstance(source, tuple):
                return jnp.where(odd, slabs[source[1]][at, :], slabs[source[0]][at, :])
            return slabs[source][at, :]

        for s, source in enumerate(sources):
            at = pl.ds(s * rows, rows)
            keys, values = part(source, pl.ds(0, rows)), part(source, pl.ds(rows, rows))
            k_hi[at, :], k_lo[at, :] = halves(keys)
            if not keeps:
                kt_hi[:, at], kt_lo[:, at] = halves(keys.T)
            v_hi[at, :], v_lo[at, :] = halves(values)
            ids = part(source, pl.ds(2 * rows, slabs[0].shape[0] - 2 * rows))
            same = jnp.where(ids == vec_ref[5:6, 0:1], F32(1), F32(0))
            count = jnp.sum(jnp.sum(same, axis=0, keepdims=True), axis=1, keepdims=True)
            first_ref[s : s + 1, :] = jnp.broadcast_to(rows - count, (1, TILE))

    ready = {}

    def load(tile):
        if tile not in ready:
            at = pl.ds(tile * TILE, TILE)
            ready[tile] = (
                *halves(q_ref[at, :] * F32(LOG2E / math.sqrt(width))),
                *halves(g_ref[at, :]),
                vec_ref[:, at],
            )
            if opens:
                high, low = halves(g_ref[at, :] * out_ref[at, :])
                ones = jnp.ones((16, width), BF16)
                delta_ref[:, at] = (dot(ones, high, NT) + dot(ones, low, NT))[0:8, :]
        return ready[tile]

    def span(tile, block):
        start, size, _ = block
        if callable(start):
            start = pl.multiple_of(start(step * steps + tile), 16)
        return pl.ds(start, size), start

    def front(tile, block):
        q_hi, q_lo, g_hi, g_lo, _ = load(tile)
        at, _ = span(tile, block)
        scores = dot(k_hi[at, :], q_hi, NT) + dot(k_lo[at, :], q_hi, NT) + dot(k_hi[at, :], q_lo, NT)
        grad_probs = dot(v_hi[at, :], g_hi, NT) + dot(v_lo[at, :], g_hi, NT) + dot(v_hi[at, :], g_lo, NT)
        return scores, grad_probs

    totals = {}

    def back(tile, block, scores, grad_probs):
        q_hi, q_lo, g_hi, g_lo, vec = load(tile)
        at, start = span(tile, block)
        size, both = block[1], block[2]
        row = lax.broadcasted_iota(jnp.int32, (size, TILE), 0).astype(F32)
        if both:
            base = lax.convert_element_type(start, F32)
            low = jnp.maximum(vec[2:3, :], first_ref[0:1, :]) - base
            allowed = (row >= low) & (row <= vec[4:5, :] - base)
        else:
            allowed = row >= jnp.maximum(vec[3:4, :], first_ref[start // rows : start // rows + 1, :])
        probs = jnp.exp2(jnp.where(allowed, scores - vec[0:1, :], F32(MASKED)))
        grad_scores = probs * (grad_probs - delta_ref[0:1, pl.ds(tile * TILE, TILE)])
        p_hi, p_lo = halves(probs)
        s_hi, s_lo = halves(grad_scores)
        dv_acc[at, :] += dot(p_hi, g_hi, NN) + dot(p_lo, g_hi, NN) + dot(p_hi, g_lo, NN)
        dk_acc[at, :] += dot(s_hi, q_hi, NN) + dot(s_lo, q_hi, NN) + dot(s_hi, q_lo, NN)
        if keeps:
            across = pl.ds(tile * TILE, TILE)
            keep_hi[at, across], keep_lo[at, across] = s_hi, s_lo
            return
        if callable(block[0]) and pads[0].shape[1] > size:
            base = pl.multiple_of(start // LANES * LANES, LANES)
            padded = pads[0].shape[1]
            at = pl.ds(base, padded)
            inner = pl.ds(pl.multiple_of(start - base, 16), size)
            for pad, half in zip(pads, (s_hi, s_lo)):
                for edge in (0, padded - LANES):
                    pad[tile, pl.ds(edge, LANES), :] = jnp.zeros((LANES, TILE), BF16)
                pad[tile, inner, :] = half
            s_hi, s_lo = pads[0][tile], pads[1][tile]
        new = dot(kt_hi[:, at], s_hi, NN) + dot(kt_lo[:, at], s_hi, NN) + dot(kt_hi[:, at], s_lo, NN)
        totals[tile] = totals[tile] + new if tile in totals else new

    work = [(tile, n) for tile in range(steps) for n in range(len(blocks))]
    coming = front(work[0][0], blocks[work[0][1]])
    for order, (tile, n) in enumerate(work):
        here = coming
        if order + 1 < len(work):
            coming = front(work[order + 1][0], blocks[work[order + 1][1]])
        back(tile, blocks[n], *here)
        if not keeps and n + 1 == len(blocks):
            at = pl.ds(tile * TILE, TILE)
            dq = totals[tile].T * F32(1 / math.sqrt(width))
            dq_ref[at, :] = dq if opens else sum_ref[at, :] + dq

    @pl.when(step == pl.num_programs(0) - 1)
    def _():
        for s, out in enumerate(outs):
            at = pl.ds(s * rows, rows)
            out[0:rows, :] = dk_acc[at, :] * F32(LN2)
            out[rows : 2 * rows, :] = dv_acc[at, :]


def attend(blocks, sources, q, g, vec, slabs, rows, *side):
    total, width = q.shape
    count = len(sources)
    keys = count * rows
    tiles = total // TILE
    opens, keeps = side[0].shape[0] == total, len(side) == 1 and side[0].shape[0] != total
    steps = math.gcd(tiles, 4 if opens or keeps else 8)
    tile_spec = pl.BlockSpec((steps * TILE, width), lambda i: (i, 0))
    lane_spec = pl.BlockSpec((8, steps * TILE), lambda i: (0, i))
    keep_spec = pl.BlockSpec((keys, steps * TILE), lambda i: (0, i))
    whole = lambda shape: pl.BlockSpec(shape, lambda i: (0, 0))
    computed = sum(b[1] for b in blocks)
    taken, given = [tile_spec], [tile_spec]
    shapes = [jax.ShapeDtypeStruct((total, width), F32)]
    if opens:
        given = [tile_spec, lane_spec]
        shapes.append(jax.ShapeDtypeStruct((8, total), F32))
    elif keeps:
        taken, given = [lane_spec], [keep_spec] * 2
        shapes = [pltpu.HBM((keys, total), BF16)] * 2
    else:
        taken = [lane_spec, tile_spec]
    return pl.pallas_call(
        functools.partial(kernel, blocks, sources, steps, rows, opens, keeps),
        grid=(tiles // steps,),
        in_specs=[tile_spec, tile_spec, lane_spec]
        + [whole(slabs[0].shape)] * len(slabs)
        + taken,
        out_specs=given + [whole((2 * rows, width))] * count,
        out_shape=shapes + [jax.ShapeDtypeStruct((2 * rows, width), F32)] * count,
        scratch_shapes=[
            pltpu.VMEM((keys, width), BF16),
            pltpu.VMEM((keys, width), BF16),
            pltpu.VMEM((width, keys), BF16),
            pltpu.VMEM((width, keys), BF16),
            pltpu.VMEM((keys, width), BF16),
            pltpu.VMEM((keys, width), BF16),
            pltpu.VMEM((keys, width), F32),
            pltpu.VMEM((keys, width), F32),
            pltpu.VMEM((8, TILE), F32),
        ]
        + [pltpu.VMEM((steps, rows + max(b[1] - rows, LANES), TILE), BF16) for b in blocks if callable(b[0])] * 2,
        compiler_params=pltpu.CompilerParams(vmem_limit_bytes=GRANT),
        cost_estimate=pl.CostEstimate(
            flops=30 * total * computed * width, bytes_accessed=12 * total * width, transcendentals=total * computed
        ),
    )(q, g, vec, *slabs, *side)


def close(steps, count, rows, *refs):
    part_ref, refs = refs[0], refs[1:]
    kept, slabs, dq_ref, kt_hi, kt_lo = refs[:count], refs[count : 2 * count], refs[-3], refs[-2], refs[-1]
    width = part_ref.shape[1]

    @pl.when(pl.program_id(0) == 0)
    def _():
        for s, slab in enumerate(slabs):
            at = pl.ds(s * rows, rows)
            kt_hi[:, at], kt_lo[:, at] = halves(slab[...].T)

    for tile in range(steps):
        at = pl.ds(tile * TILE, TILE)
        total = None
        for n in range(0, count, 2):
            keys = pl.ds(n * rows, 2 * rows)
            high, low = kept[n][:, at], kept[n + 1][:, at]
            new = dot(kt_hi[:, keys], high, NN) + dot(kt_lo[:, keys], high, NN) + dot(kt_hi[:, keys], low, NN)
            total = new if total is None else total + new
        dq_ref[at, :] = part_ref[at, :] + total.T * F32(1 / math.sqrt(width))


def query_grads(part, kept, slabs, rows):
    total, width = part.shape
    tiles = total // TILE
    steps = math.gcd(tiles, 4)
    count = len(slabs)
    tile_spec = pl.BlockSpec((steps * TILE, width), lambda i: (i, 0))
    return pl.pallas_call(
        functools.partial(close, steps, count, rows),
        grid=(tiles // steps,),
        in_specs=[tile_spec]
        + [pl.BlockSpec((2 * rows, steps * TILE), lambda i: (0, i))] * count
        + [pl.BlockSpec((rows, width), lambda i: (0, 0))] * count,
        out_specs=tile_spec,
        out_shape=jax.ShapeDtypeStruct((total, width), F32),
        scratch_shapes=[pltpu.VMEM((width, count * rows), BF16)] * 2,
        compiler_params=pltpu.CompilerParams(vmem_limit_bytes=GRANT),
        cost_estimate=pl.CostEstimate(
            flops=6 * total * count * rows * width, bytes_accessed=4 * total * (count * rows + 2 * width), transcendentals=0
        ),
    )(part, *kept, *slabs)


def program(queries, key_rows, value_rows, forward_out, out_grad, log_norm, doc_ids):
    rows, heads, width = queries.shape
    reach = WIN // rows
    ids = doc_ids
    if lax.axis_size("head") > 1:
        gather = functools.partial(lax.all_gather, axis_name="head", axis=0, tiled=True)
        key_rows, value_rows = gather(key_rows), gather(value_rows)
        ids = gather(ids.astype(F32)).astype(jnp.int32)
    own = packed(key_rows, value_rows, ids)
    odd = lax.axis_index("seq") % 2 == 1

    mine, other = {0: own}, {}
    for distance in range(reach, 0, -2):
        mine[distance] = shifted(own, "seq", distance)
    for distance in range(reach, -1, -2):
        other[distance] = swapped(mine[distance], "seq")

    token = jnp.arange(rows, dtype=F32)
    before = jnp.sum((ids[None, :] < ids[:, None]).astype(F32), axis=1)
    first = before == 0
    per_token = jnp.stack(
        [
            jnp.where(first, token + 1, rows + before),
            jnp.where(first, 0.0, 1e9),
            token + rows,
            ids.astype(F32) + 1,
            jnp.broadcast_to(odd.astype(F32), (rows,)),
        ]
    )
    spread = jnp.broadcast_to(per_token[:, :, None], (5, rows, heads)).reshape(5, rows * heads)
    scaled = (log_norm * F32(LOG2E)).reshape(1, -1)
    blank = jnp.zeros((1, rows * heads), F32)
    vec = jnp.concatenate([scaled, blank, spread, blank], axis=0)

    q = queries.reshape(rows * heads, width)
    g = out_grad.reshape(rows * heads, width)
    tokens = TILE // heads
    unit = max(tokens, 16)
    edges = ((lambda i: (i * tokens) // unit * unit, rows + unit, True), (2 * rows, rows, False))
    out = forward_out.reshape(rows * heads, width)
    here = lambda x: pltpu.with_memory_space_constraint(x, pltpu.HBM)
    dq, delta, far, own_part, cross = attend(
        edges, (0, 1, (2, 3)), here(q), here(g), vec, [mine[reach], own, other[reach], other[0]], rows, here(out)
    )
    cross = swapped(cross, "seq")
    returned = [shifted(far + jnp.where(odd, cross, 0.0), "seq", -reach)]
    returned.append(jnp.where(odd, 0.0, cross))
    blocks = ((0, rows, False), (rows, rows, False))
    kept, slabs = [], []
    for d in range(reach - 2, 0, -2):
        if d > KEPT:
            dq, part, hand = attend(blocks, (0, 1), q, g, vec, [mine[d], other[d]], rows, delta, dq)
        else:
            high, low, part, hand = attend(blocks, (0, 1), q, g, vec, [mine[d], other[d]], rows, delta)
            kept += [high, low]
            slabs += [mine[d], other[d]]
        hand = swapped(hand, "seq")
        returned.append(shifted(part + hand, "seq", -d))
    dq = query_grads(here(dq), [here(x) for x in kept], [here(x) for x in slabs], rows)
    keys_grad = sum([part[:rows] for part in returned], own_part[:rows])
    values_grad = sum([part[rows:] for part in returned], own_part[rows:])
    if lax.axis_size("head") > 1:
        keys_grad, values_grad = (
            lax.psum_scatter(x, "head", scatter_dimension=0, tiled=True) for x in (keys_grad, values_grad)
        )
    return dq.reshape(rows, heads, width), keys_grad, values_grad


def solution(mesh):
    in_specs = (
        P("seq", "head", None),
        P(("seq", "head"), None),
        P(("seq", "head"), None),
        P("seq", "head", None),
        P("seq", "head", None),
        P("seq", "head"),
        P(("seq", "head")),
    )
    out_specs = (P("seq", "head", None), P(("seq", "head"), None), P(("seq", "head"), None))
    return jax.shard_map(program, mesh=mesh, in_specs=in_specs, out_specs=out_specs, check_vma=False)
```

```python
import functools
import math

import jax
import jax.numpy as jnp
from jax import lax
from jax.experimental import pallas as pl
from jax.experimental.pallas import tpu as pltpu
from jax.sharding import PartitionSpec as P


WIN = 2048
TILE = 256
LANES = 128
LOG2E = math.log2(math.e)
KEPT = 4
GRANT = 24 * 1024 * 1024
LN2 = math.log(2.0)
MASKED = -1e30
NN = (((1,), (0,)), ((), ()))
NT = (((1,), (1,)), ((), ()))
F32 = jnp.float32
BF16 = jnp.bfloat16


def shifted(value, axis, steps):
    count = lax.axis_size(axis)
    leading, last = (max(0, -steps), min(count, count - steps))
    return lax.ppermute(value, axis, [(source, source + steps) for source in range(leading, last)])


def swapped(value, axis):
    count = lax.axis_size(axis)
    return lax.ppermute(value, axis, [(source, source ^ 1) for source in range(count)])


def dot(a, b, dims):
    return lax.dot_general(a, b, dims, preferred_element_type=F32)


def halves(x):
    high = x.astype(BF16)
    return high, (x - high.astype(F32)).astype(BF16)


def pack(k_ref, v_ref, ids_ref, out_ref):
    rows = k_ref.shape[0]
    out_ref[0:rows, :] = k_ref[...]
    out_ref[rows : 2 * rows, :] = v_ref[...]
    out_ref[2 * rows :, :] = jnp.zeros_like(out_ref[2 * rows :, :])
    out_ref[2 * rows : 2 * rows + ids_ref.shape[0], :] = ids_ref[...].astype(F32) + F32(1)


def packed(keys, values, ids):
    rows, width = keys.shape
    lines = pl.cdiv(rows, width)
    lined = jnp.pad(ids, (0, lines * width - rows), constant_values=-1).reshape(lines, width)
    return pl.pallas_call(
        pack, out_shape=jax.ShapeDtypeStruct((2 * rows + 8 * pl.cdiv(lines, 8), width), F32)
    )(keys, values, lined)


def kernel(blocks, sources, steps, rows, opens, keeps, *refs):
    operands = 1 + max(max(s) if isinstance(s, tuple) else s for s in sources)
    q_ref, g_ref, vec_ref, *rest = refs
    slabs, rest = rest[:operands], rest[operands:]
    if opens:
        out_ref, dq_ref, delta_ref, *rest = rest
    elif keeps:
        delta_ref, keep_hi, keep_lo, *rest = rest
    else:
        delta_ref, sum_ref, dq_ref, *rest = rest
    outs, rest = rest[: len(sources)], rest[len(sources) :]
    k_hi, k_lo, kt_hi, kt_lo, v_hi, v_lo, dk_acc, dv_acc, first_ref, *pads = rest
    step = pl.program_id(0)
    width = q_ref.shape[1]

    @pl.when(step == 0)
    def _():
        dk_acc[...] = jnp.zeros_like(dk_acc)
        dv_acc[...] = jnp.zeros_like(dv_acc)
        odd = vec_ref[6:7, 0:1] > 0.5

        def part(source, at):
            if isinstance(source, tuple):
                return jnp.where(odd, slabs[source[1]][at, :], slabs[source[0]][at, :])
            return slabs[source][at, :]

        for s, source in enumerate(sources):
            at = pl.ds(s * rows, rows)
            keys, values = part(source, pl.ds(0, rows)), part(source, pl.ds(rows, rows))
            k_hi[at, :], k_lo[at, :] = halves(keys)
            if not keeps:
                kt_hi[:, at], kt_lo[:, at] = halves(keys.T)
            v_hi[at, :], v_lo[at, :] = halves(values)
            ids = part(source, pl.ds(2 * rows, slabs[0].shape[0] - 2 * rows))
            same = jnp.where(ids == vec_ref[5:6, 0:1], F32(1), F32(0))
            count = jnp.sum(jnp.sum(same, axis=0, keepdims=True), axis=1, keepdims=True)
            first_ref[s : s + 1, :] = jnp.broadcast_to(rows - count, (1, TILE))

    ready = {}

    def load(tile):
        if tile not in ready:
            at = pl.ds(tile * TILE, TILE)
            ready[tile] = (
                *halves(q_ref[at, :] * F32(LOG2E / math.sqrt(width))),
                *halves(g_ref[at, :]),
                vec_ref[:, at],
            )
            if opens:
                both = (g_ref[at, :] * out_ref[at, :]).T
                delta_ref[:, at] = jnp.broadcast_to(jnp.sum(both, axis=0, keepdims=True), (8, TILE))
        return ready[tile]

    def span(tile, block):
        start, size, _ = block
        if callable(start):
            start = pl.multiple_of(start(step * steps + tile), 16)
        return pl.ds(start, size), start

    def front(tile, block):
        q_hi, q_lo, g_hi, g_lo, _ = load(tile)
        at, _ = span(tile, block)
        scores = dot(k_hi[at, :], q_hi, NT) + dot(k_lo[at, :], q_hi, NT) + dot(k_hi[at, :], q_lo, NT)
        grad_probs = dot(v_hi[at, :], g_hi, NT) + dot(v_lo[at, :], g_hi, NT) + dot(v_hi[at, :], g_lo, NT)
        return scores, grad_probs

    totals = {}

    def back(tile, block, scores, grad_probs):
        q_hi, q_lo, g_hi, g_lo, vec = load(tile)
        at, start = span(tile, block)
        size, both = block[1], block[2]
        row = lax.broadcasted_iota(jnp.int32, (size, TILE), 0).astype(F32)
        if both:
            base = lax.convert_element_type(start, F32)
            low = jnp.maximum(vec[2:3, :], first_ref[0:1, :]) - base
            allowed = (row >= low) & (row <= vec[4:5, :] - base)
        else:
            allowed = row >= jnp.maximum(vec[3:4, :], first_ref[start // rows : start // rows + 1, :])
        probs = jnp.exp2(jnp.where(allowed, scores - vec[0:1, :], F32(MASKED)))
        grad_scores = probs * (grad_probs - delta_ref[0:1, pl.ds(tile * TILE, TILE)])
        p_hi, p_lo = halves(probs)
        s_hi, s_lo = halves(grad_scores)
        dv_acc[at, :] += dot(p_hi, g_hi, NN) + dot(p_lo, g_hi, NN) + dot(p_hi, g_lo, NN)
        dk_acc[at, :] += dot(s_hi, q_hi, NN) + dot(s_lo, q_hi, NN) + dot(s_hi, q_lo, NN)
        if keeps:
            across = pl.ds(tile * TILE, TILE)
            keep_hi[at, across], keep_lo[at, across] = s_hi, s_lo
            return
        if callable(block[0]) and pads[0].shape[1] > size:
            base = pl.multiple_of(start // LANES * LANES, LANES)
            padded = pads[0].shape[1]
            at = pl.ds(base, padded)
            inner = pl.ds(pl.multiple_of(start - base, 16), size)
            for pad, half in zip(pads, (s_hi, s_lo)):
                for edge in (0, padded - LANES):
                    pad[tile, pl.ds(edge, LANES), :] = jnp.zeros((LANES, TILE), BF16)
                pad[tile, inner, :] = half
            s_hi, s_lo = pads[0][tile], pads[1][tile]
        new = dot(kt_hi[:, at], s_hi, NN) + dot(kt_lo[:, at], s_hi, NN) + dot(kt_hi[:, at], s_lo, NN)
        totals[tile] = totals[tile] + new if tile in totals else new

    work = [(tile, n) for tile in range(steps) for n in range(len(blocks))]
    coming = front(work[0][0], blocks[work[0][1]])
    for order, (tile, n) in enumerate(work):
        here = coming
        if order + 1 < len(work):
            coming = front(work[order + 1][0], blocks[work[order + 1][1]])
        back(tile, blocks[n], *here)
        if not keeps and n + 1 == len(blocks):
            at = pl.ds(tile * TILE, TILE)
            dq = totals[tile].T * F32(1 / math.sqrt(width))
            dq_ref[at, :] = dq if opens else sum_ref[at, :] + dq

    @pl.when(step == pl.num_programs(0) - 1)
    def _():
        for s, out in enumerate(outs):
            at = pl.ds(s * rows, rows)
            out[0:rows, :] = dk_acc[at, :] * F32(LN2)
            out[rows : 2 * rows, :] = dv_acc[at, :]


def attend(blocks, sources, q, g, vec, slabs, rows, *side):
    total, width = q.shape
    count = len(sources)
    keys = count * rows
    tiles = total // TILE
    opens, keeps = side[0].shape[0] == total, len(side) == 1 and side[0].shape[0] != total
    steps = math.gcd(tiles, 4 if opens or keeps else 8)
    tile_spec = pl.BlockSpec((steps * TILE, width), lambda i: (i, 0))
    lane_spec = pl.BlockSpec((8, steps * TILE), lambda i: (0, i))
    keep_spec = pl.BlockSpec((keys, steps * TILE), lambda i: (0, i))
    whole = lambda shape: pl.BlockSpec(shape, lambda i: (0, 0))
    computed = sum(b[1] for b in blocks)
    taken, given = [tile_spec], [tile_spec]
    shapes = [jax.ShapeDtypeStruct((total, width), F32)]
    if opens:
        given = [tile_spec, lane_spec]
        shapes.append(jax.ShapeDtypeStruct((8, total), F32))
    elif keeps:
        taken, given = [lane_spec], [keep_spec] * 2
        shapes = [pltpu.HBM((keys, total), BF16)] * 2
    else:
        taken = [lane_spec, tile_spec]
    return pl.pallas_call(
        functools.partial(kernel, blocks, sources, steps, rows, opens, keeps),
        grid=(tiles // steps,),
        in_specs=[tile_spec, tile_spec, lane_spec]
        + [whole(slabs[0].shape)] * len(slabs)
        + taken,
        out_specs=given + [whole((2 * rows, width))] * count,
        out_shape=shapes + [jax.ShapeDtypeStruct((2 * rows, width), F32)] * count,
        scratch_shapes=[
            pltpu.VMEM((keys, width), BF16),
            pltpu.VMEM((keys, width), BF16),
            pltpu.VMEM((width, keys), BF16),
            pltpu.VMEM((width, keys), BF16),
            pltpu.VMEM((keys, width), BF16),
            pltpu.VMEM((keys, width), BF16),
            pltpu.VMEM((keys, width), F32),
            pltpu.VMEM((keys, width), F32),
            pltpu.VMEM((8, TILE), F32),
        ]
        + [pltpu.VMEM((steps, rows + max(b[1] - rows, LANES), TILE), BF16) for b in blocks if callable(b[0])] * 2,
        compiler_params=pltpu.CompilerParams(vmem_limit_bytes=GRANT),
        cost_estimate=pl.CostEstimate(
            flops=30 * total * computed * width, bytes_accessed=12 * total * width, transcendentals=total * computed
        ),
    )(q, g, vec, *slabs, *side)


def close(steps, count, rows, *refs):
    part_ref, refs = refs[0], refs[1:]
    kept, slabs, dq_ref, kt_hi, kt_lo = refs[:count], refs[count : 2 * count], refs[-3], refs[-2], refs[-1]
    width = part_ref.shape[1]

    @pl.when(pl.program_id(0) == 0)
    def _():
        for s, slab in enumerate(slabs):
            at = pl.ds(s * rows, rows)
            kt_hi[:, at], kt_lo[:, at] = halves(slab[...].T)

    for tile in range(steps):
        at = pl.ds(tile * TILE, TILE)
        total = None
        for n in range(0, count, 2):
            keys = pl.ds(n * rows, 2 * rows)
            high, low = kept[n][:, at], kept[n + 1][:, at]
            new = dot(kt_hi[:, keys], high, NN) + dot(kt_lo[:, keys], high, NN) + dot(kt_hi[:, keys], low, NN)
            total = new if total is None else total + new
        dq_ref[at, :] = part_ref[at, :] + total.T * F32(1 / math.sqrt(width))


def query_grads(part, kept, slabs, rows):
    total, width = part.shape
    tiles = total // TILE
    steps = math.gcd(tiles, 4)
    count = len(slabs)
    tile_spec = pl.BlockSpec((steps * TILE, width), lambda i: (i, 0))
    return pl.pallas_call(
        functools.partial(close, steps, count, rows),
        grid=(tiles // steps,),
        in_specs=[tile_spec]
        + [pl.BlockSpec((2 * rows, steps * TILE), lambda i: (0, i))] * count
        + [pl.BlockSpec((rows, width), lambda i: (0, 0))] * count,
        out_specs=tile_spec,
        out_shape=jax.ShapeDtypeStruct((total, width), F32),
        scratch_shapes=[pltpu.VMEM((width, count * rows), BF16)] * 2,
        compiler_params=pltpu.CompilerParams(vmem_limit_bytes=GRANT),
        cost_estimate=pl.CostEstimate(
            flops=6 * total * count * rows * width, bytes_accessed=4 * total * (count * rows + 2 * width), transcendentals=0
        ),
    )(part, *kept, *slabs)


def program(queries, key_rows, value_rows, forward_out, out_grad, log_norm, doc_ids):
    rows, heads, width = queries.shape
    reach = WIN // rows
    ids = doc_ids
    if lax.axis_size("head") > 1:
        gather = functools.partial(lax.all_gather, axis_name="head", axis=0, tiled=True)
        key_rows, value_rows = gather(key_rows), gather(value_rows)
        ids = gather(ids.astype(F32)).astype(jnp.int32)
    own = packed(key_rows, value_rows, ids)
    odd = lax.axis_index("seq") % 2 == 1

    mine, other = {0: own}, {}
    for distance in range(reach, 0, -2):
        mine[distance] = shifted(own, "seq", distance)
    for distance in range(reach, -1, -2):
        other[distance] = swapped(mine[distance], "seq")

    token = jnp.arange(rows, dtype=F32)
    before = jnp.sum((ids[None, :] < ids[:, None]).astype(F32), axis=1)
    first = before == 0
    per_token = jnp.stack(
        [
            jnp.where(first, token + 1, rows + before),
            jnp.where(first, 0.0, 1e9),
            token + rows,
            ids.astype(F32) + 1,
            jnp.broadcast_to(odd.astype(F32), (rows,)),
        ]
    )
    spread = jnp.broadcast_to(per_token[:, :, None], (5, rows, heads)).reshape(5, rows * heads)
    scaled = (log_norm * F32(LOG2E)).reshape(1, -1)
    blank = jnp.zeros((1, rows * heads), F32)
    vec = jnp.concatenate([scaled, blank, spread, blank], axis=0)

    q = queries.reshape(rows * heads, width)
    g = out_grad.reshape(rows * heads, width)
    tokens = TILE // heads
    unit = max(tokens, 16)
    edges = ((lambda i: (i * tokens) // unit * unit, rows + unit, True), (2 * rows, rows, False))
    out = forward_out.reshape(rows * heads, width)
    here = lambda x: pltpu.with_memory_space_constraint(x, pltpu.HBM)
    dq, delta, far, own_part, cross = attend(
        edges, (0, 1, (2, 3)), here(q), here(g), vec, [mine[reach], own, other[reach], other[0]], rows, here(out)
    )
    cross = swapped(cross, "seq")
    returned = [shifted(far + jnp.where(odd, cross, 0.0), "seq", -reach)]
    returned.append(jnp.where(odd, 0.0, cross))
    blocks = ((0, rows, False), (rows, rows, False))
    kept, slabs = [], []
    for d in range(reach - 2, 0, -2):
        if d > KEPT:
            dq, part, hand = attend(blocks, (0, 1), q, g, vec, [mine[d], other[d]], rows, delta, dq)
        else:
            high, low, part, hand = attend(blocks, (0, 1), q, g, vec, [mine[d], other[d]], rows, delta)
            kept += [high, low]
            slabs += [mine[d], other[d]]
        hand = swapped(hand, "seq")
        returned.append(shifted(part + hand, "seq", -d))
    dq = query_grads(here(dq), [here(x) for x in kept], [here(x) for x in slabs], rows)
    keys_grad = sum([part[:rows] for part in returned], own_part[:rows])
    values_grad = sum([part[rows:] for part in returned], own_part[rows:])
    if lax.axis_size("head") > 1:
        keys_grad, values_grad = (
            lax.psum_scatter(x, "head", scatter_dimension=0, tiled=True) for x in (keys_grad, values_grad)
        )
    return dq.reshape(rows, heads, width), keys_grad, values_grad


def solution(mesh):
    in_specs = (
        P("seq", "head", None),
        P(("seq", "head"), None),
        P(("seq", "head"), None),
        P("seq", "head", None),
        P("seq", "head", None),
        P("seq", "head"),
        P(("seq", "head")),
    )
    out_specs = (P("seq", "head", None), P(("seq", "head"), None), P(("seq", "head"), None))
    return jax.shard_map(program, mesh=mesh, in_specs=in_specs, out_specs=out_specs, check_vma=False)
```
